32 devices in a mesh: dp: 8 (over z, x), seq: 4 (over y, core).
Axes of the slice: x: 2, y: 2, z: 4, core: 2. Of those that a mesh axis runs over, the one named last changes fastest.
Arguments:
- query_rows: bfloat16 [4096, 4096], P(('dp', 'seq')), may hold values from -60 to 60
- key_rows: bfloat16 [4096, 4096], P(('dp', 'seq')), may hold values from -5 to 5
- value_rows: bfloat16 [4096, 4096], P(('dp', 'seq')), may hold values from -12 to 12
- seg_ids: int32 [4096], P(('dp', 'seq')), may hold values from 0 to 15, as said below
- timesteps: int32 [16], replicated, may hold values from 0 to 999
- w_mod: bfloat16 [256, 4096], replicated, may hold values from -0.375 to 0.375
Outputs:
- mixed_rows: bfloat16 [4096, 4096], P(('dp', 'seq'))
The draws below stay inside these ranges and needn't reach their ends.
Inputs may be any that keep to these rules, and one draw needn't show every extreme that they name: A row's bin is seg_ids // 2, a number below the size of dp. The 128 rows of one device hold at most 32 rows of any one bin, and for every index of seq some bin holds exactly 32 rows on each device of that index. Rows of one sample lie on many devices.
All inputs are finite; a program needn't handle non-finite values.
Results may differ from the reference program's by a relative error of at most 0.0058.
Values may be sent and summed in bfloat16 or wider, within the bound.
A program may use at most 128 MiB of HBM per device.

```python
import math
import jax
import jax.numpy as jnp
from jax import lax

HEADS = 32
HEAD_DIM = 128
D = 4096
FREQ = 256
TOK_DEV = 128
SEG_BIN = 2
BIN_SLOTS = 1024
ROWS = 4096
SAMPLES = 16
N_DP = 8
N_SEQ = 4


def seg_layout(key):
    devices = N_DP * N_SEQ
    mean_rows = TOK_DEV // N_DP
    key_base = jax.random.fold_in(key, 11)
    full_bins = jax.random.randint(jax.random.fold_in(key_base, 1), (N_SEQ,), 0, N_DP)

    def one_device(device):
        dev_key = jax.random.fold_in(key_base, 100 + device)
        sub_keys = jax.random.split(dev_key, 4)
        full_bin = full_bins[device % N_SEQ]
        bin_scores = jax.random.randint(sub_keys[0], (N_DP,), 0, 1 << 16) * N_DP + jnp.arange(N_DP)
        bin_scores = jnp.where(jnp.arange(N_DP) == full_bin, -1, bin_scores)
        bin_order = jnp.argsort(bin_scores)
        shifts = jax.random.randint(sub_keys[1], (N_DP // 2,), 0, mean_rows + 1)
        shifts = shifts.at[0].set(mean_rows)
        count_sorted = jnp.stack([mean_rows + shifts, mean_rows - shifts], axis=1).reshape(-1)
        bounds = jnp.cumsum(count_sorted)
        positions = jnp.arange(TOK_DEV)
        bin_slot = jnp.sum((positions[:, None] >= bounds[None, :]).astype(jnp.int32), axis=1)
        row_bins = bin_order[bin_slot]
        groups = jax.random.randint(sub_keys[2], (TOK_DEV,), 0, SEG_BIN)
        groups = groups.at[1].set(groups[0])
        sample_ids = row_bins * SEG_BIN + groups
        shuffle_scores = jax.random.randint(sub_keys[3], (TOK_DEV,), 0, 1 << 16) * TOK_DEV + positions
        shuffle = jnp.argsort(shuffle_scores)
        inverse = jnp.argsort(shuffle)
        return (sample_ids[shuffle], inverse[0], inverse[1])
    return jax.vmap(one_device)(jnp.arange(devices))


def draw_seg_ids(key, part):
    sample_ids, first_row, second_row = seg_layout(key)
    return sample_ids.reshape(-1).astype(jnp.int32)


def draw_key_rows(key, part):
    devices = N_DP * N_SEQ
    row_data = jnp.clip(jax.random.normal(jax.random.fold_in(key, 29), (devices, TOK_DEV, D), jnp.float32), -4.5, 4.5)
    return row_data.reshape(devices * TOK_DEV, D).astype(jnp.bfloat16)


def draw_query_rows(key, part):
    devices = N_DP * N_SEQ
    key_base = jax.random.fold_in(key, 31)
    row_data = jnp.clip(jax.random.normal(key_base, (devices, TOK_DEV, D), jnp.float32), -4.5, 4.5)
    return row_data.reshape(devices * TOK_DEV, D).astype(jnp.bfloat16)


def plant(drawn, key, least, top_value):
    dims = drawn.shape
    index_at = [jax.random.randint(jax.random.fold_in(key, axis), (), 0, dims[axis]) for axis in range(len(dims))]
    drawn = drawn.at[tuple(index_at)].set(least)
    longest = dims.index(max(dims))
    index_at[longest] = (index_at[longest] + 1) % dims[longest]
    return drawn.at[tuple(index_at)].set(top_value)


def shard_levels(own_key, dims, cuts, smallest, top_value):
    def one(dim, blocks):
        steps = jax.random.uniform(jax.random.fold_in(jax.random.fold_in(own_key, 6), dim), (blocks,), jnp.float32, smallest / len(cuts), top_value / len(cuts))
        return jnp.repeat(jnp.exp(steps), dims[dim] // blocks).reshape((-1,) + (1,) * (len(dims) - dim - 1))

    loudness = one(*cuts[0])
    for cut in cuts[1:]:
        loudness = loudness * one(*cut)
    return loudness


def scatter_about(rng, extent, deviation, limit, pieces=(), kind=jnp.bfloat16):
    factor_of = shard_levels(rng, extent, pieces, -0.22, 0.18) if pieces else 1.0
    values = jax.random.normal(rng, extent, jnp.float32) * deviation * factor_of
    return jnp.minimum(jnp.maximum(values, -limit), limit).astype(kind)


def setup_inputs(seed: int = 0) -> dict:
    arg_keys = jax.random.split(jax.random.key(seed), 7)
    query_rows = draw_query_rows(jax.random.fold_in(arg_keys[6], 71), 0)
    key_rows = draw_key_rows(jax.random.fold_in(arg_keys[6], 71), 0)
    value_rows = scatter_about(arg_keys[2], (ROWS, D), 2.0, 12.0, ((0, 32),))
    seg_ids = draw_seg_ids(jax.random.fold_in(arg_keys[6], 71), 0)
    timesteps = plant(jax.random.randint(arg_keys[4], (SAMPLES,), 0, 1000), jax.random.fold_in(arg_keys[4], 1), 0, 999).astype(jnp.int32)
    w_mod = scatter_about(arg_keys[5], (FREQ, D), FREQ ** -0.5, 0.375)
    return dict(query_rows=query_rows, key_rows=key_rows, value_rows=value_rows, seg_ids=seg_ids, timesteps=timesteps, w_mod=w_mod)


def scale_rows_table(timesteps, w_mod):
    half_freq = FREQ // 2
    frequencies = jnp.exp(-math.log(10000.0) * jnp.arange(half_freq, dtype=jnp.float32) / half_freq)
    angles = timesteps.astype(jnp.float32)[:, None] * frequencies[None, :]
    embedding = jnp.concatenate([jnp.cos(angles), jnp.sin(angles)], axis=1)
    activated = jax.nn.silu(embedding).astype(jnp.bfloat16)
    return jnp.dot(activated, w_mod, preferred_element_type=jnp.float32)

def attend_bin(query_part, key_part, value_part, sample_ids):
    score_scale = 1.0 / math.sqrt(HEAD_DIM)
    same_sample = sample_ids[:, None] == sample_ids[None, :]

    def one_head(head_start):
        head_query = lax.dynamic_slice_in_dim(query_part, head_start, HEAD_DIM, 1)
        head_key = lax.dynamic_slice_in_dim(key_part, head_start, HEAD_DIM, 1)
        head_value = lax.dynamic_slice_in_dim(value_part, head_start, HEAD_DIM, 1)
        scores = jnp.dot(head_query, head_key.T, preferred_element_type=jnp.float32) * score_scale
        scores = jnp.where(same_sample, scores, -1e+30)
        row_max = lax.optimization_barrier(jnp.max(scores, axis=1, keepdims=True))
        weights = jnp.exp(scores - row_max)
        soft_probs = (weights / lax.optimization_barrier(jnp.sum(weights, axis=1, keepdims=True))).astype(jnp.bfloat16)
        return jnp.dot(soft_probs, head_value, preferred_element_type=jnp.float32).astype(jnp.bfloat16)
    head_starts = jnp.arange(HEADS, dtype=jnp.int32) * HEAD_DIM
    per_head = lax.map(one_head, head_starts)
    return jnp.transpose(per_head, (1, 0, 2)).reshape(sample_ids.shape[0], D)

def reference(query_rows, key_rows, value_rows, seg_ids, timesteps, w_mod):
    row_total = query_rows.shape[0]
    row_bins = (seg_ids // SEG_BIN).astype(jnp.int32)
    row_order = jnp.argsort(row_bins, stable=True).astype(jnp.int32)
    counts = lax.optimization_barrier(jnp.sum((row_bins[None, :] == jnp.arange(N_DP, dtype=jnp.int32)[:, None]).astype(jnp.int32), axis=1))
    starts = (jnp.cumsum(counts) - counts).astype(jnp.int32)
    order_padded = jnp.concatenate([row_order, jnp.full((BIN_SLOTS,), row_total, jnp.int32)])
    zero_row = jnp.zeros((1, D), jnp.bfloat16)
    query_padded = jnp.concatenate([query_rows, zero_row])
    key_padded = jnp.concatenate([key_rows, zero_row])
    value_padded = jnp.concatenate([value_rows, zero_row])
    ids_padded = jnp.concatenate([seg_ids, jnp.full((1,), -1, jnp.int32)])

    def one_bin(bin_number):
        picked = lax.dynamic_slice_in_dim(order_padded, starts[bin_number], BIN_SLOTS)
        live_slots = jnp.arange(BIN_SLOTS) < counts[bin_number]
        picked = jnp.where(live_slots, picked, row_total).astype(jnp.int32)
        attended = attend_bin(query_padded[picked], key_padded[picked], value_padded[picked], ids_padded[picked])
        return (picked, attended)
    picked_all, attended_all = lax.map(one_bin, jnp.arange(N_DP, dtype=jnp.int32))
    attended = jnp.zeros((row_total + 1, D), jnp.bfloat16)
    attended = attended.at[picked_all.reshape(-1)].set(attended_all.reshape(-1, D))[:row_total]
    scale_table = scale_rows_table(timesteps, w_mod)
    row_scales = scale_table[seg_ids]
    return (attended.astype(jnp.float32) * (1.0 + row_scales)).astype(jnp.bfloat16)
```

```python
import functools
import math

import jax
import jax.numpy as jnp
from jax import lax
from jax.experimental import pallas as pl
from jax.experimental.pallas import tpu as pltpu
from jax.sharding import PartitionSpec as P

HEAD_DIM = 128
FREQ = 256
SEG_BIN = 2


def for_sending(value):
    return jax.tree.map(lambda a: a.astype(jnp.bfloat16) if a.dtype == jnp.float32 else a, value)


def scale_rows_table(timesteps, w_mod):
    half_freq = FREQ // 2
    frequencies = jnp.exp(-math.log(10000.0) * jnp.arange(half_freq, dtype=jnp.float32) / half_freq)
    angles = timesteps.astype(jnp.float32)[:, None] * frequencies[None, :]
    embedding = jnp.concatenate([jnp.cos(angles), jnp.sin(angles)], axis=1)
    activated = jax.nn.silu(embedding).astype(jnp.bfloat16)
    return jnp.dot(activated, w_mod, preferred_element_type=jnp.float32)


def slot_places(row_bins, bin_count, capacity):
    bin_hits = (row_bins[:, None] == jnp.arange(bin_count, dtype=jnp.int32)[None, :]).astype(
        jnp.int32
    )
    ranks = jnp.cumsum(bin_hits, axis=0) - bin_hits
    slot_rank = jnp.sum(ranks * bin_hits, axis=1)
    target = row_bins * capacity + slot_rank
    return jnp.arange(bin_count * capacity, dtype=jnp.int32)[:, None] == target[None, :]


def slot_ids_of(placement, sample_ids):
    return jnp.sum(jnp.where(placement, sample_ids[None, :] + 1, 0), axis=1) - 1


def attend_slots(query_part, key_part, value_part, sample_ids):
    length, row_width = query_part.shape
    head_count = row_width // HEAD_DIM
    block_rows = min(512, length)
    score_scale = 1.0 / math.sqrt(HEAD_DIM)
    query_blocks = query_part.reshape(length // block_rows, block_rows, head_count, HEAD_DIM)
    key_heads = key_part.reshape(length, head_count, HEAD_DIM)
    value_heads = value_part.reshape(length, head_count, HEAD_DIM)
    id_blocks = sample_ids.reshape(length // block_rows, block_rows)

    def one_block(block_pair):
        query_block, query_ids = block_pair
        scores = (
            jnp.einsum("qhd,khd->hqk", query_block, key_heads, preferred_element_type=jnp.float32)
            * score_scale
        )
        same_sample = query_ids[:, None] == sample_ids[None, :]
        scores = jnp.where(same_sample[None], scores, -1e30)
        row_max = jnp.max(scores, axis=2, keepdims=True)
        weights = jnp.exp(scores - row_max)
        soft_probs = (weights / jnp.sum(weights, axis=2, keepdims=True)).astype(jnp.bfloat16)
        block_out = jnp.einsum(
            "hqk,khd->qhd", soft_probs, value_heads, preferred_element_type=jnp.float32
        )
        return block_out.astype(jnp.bfloat16).reshape(block_rows, row_width)

    return lax.map(one_block, (query_blocks, id_blocks)).reshape(length, row_width)


def place_rows(place_mask, arrays):
    return tuple(
        (
            jnp.dot(place_mask, single, preferred_element_type=jnp.float32).astype(jnp.bfloat16)
            for single in arrays
        )
    )


def routed_shards(query_rows, key_rows, value_rows, seg_ids, timesteps, w_mod):
    dp_count = lax.axis_size("dp")
    seq_count = lax.axis_size("seq")
    row_count = query_rows.shape[0]
    capacity = 2 * row_count // dp_count
    ids_tiled = jnp.broadcast_to(seg_ids[:, None], (row_count, seq_count))
    group_ids = lax.all_to_all(ids_tiled, "seq", split_axis=1, concat_axis=0, tiled=True).reshape(
        -1
    )
    head_parts = (
        lax.all_to_all(query_rows, "seq", split_axis=1, concat_axis=0, tiled=True),
        lax.all_to_all(key_rows, "seq", split_axis=1, concat_axis=0, tiled=True),
        lax.all_to_all(value_rows, "seq", split_axis=1, concat_axis=0, tiled=True),
    )
    placement = slot_places(group_ids // SEG_BIN, dp_count, seq_count * capacity)
    place_mask = placement.astype(jnp.bfloat16)
    slotted = place_rows(place_mask, head_parts)
    bin_ids = lax.all_to_all(
        slot_ids_of(placement, group_ids), "dp", split_axis=0, concat_axis=0, tiled=True
    )
    bin_query, bin_key, bin_value = jax.tree.map(
        lambda part, own: part.astype(own.dtype),
        lax.all_to_all(for_sending(slotted), "dp", split_axis=0, concat_axis=0, tiled=True),
        slotted,
    )
    attended = attend_slots(bin_query, bin_key, bin_value, bin_ids)
    returned = lax.all_to_all(attended, "dp", split_axis=0, concat_axis=0, tiled=True)
    unslotted = jnp.dot(place_mask.T, returned, preferred_element_type=jnp.float32).astype(
        jnp.bfloat16
    )
    home_rows = lax.all_to_all(unslotted, "seq", split_axis=0, concat_axis=1, tiled=True)
    scale_table = scale_rows_table(timesteps, w_mod)
    lookup = (
        seg_ids[:, None] == jnp.arange(scale_table.shape[0], dtype=jnp.int32)[None, :]
    ).astype(jnp.float32)
    row_scales = jnp.dot(
        lookup, scale_table, precision=lax.Precision.HIGHEST, preferred_element_type=jnp.float32
    )
    return (home_rows.astype(jnp.float32) * (1.0 + row_scales)).astype(jnp.bfloat16)


EXCLUDED = float(1 << 20)
NT = (((1,), (1,)), ((), ()))
TN = (((0,), (0,)), ((), ()))


def head_kernel(
    sizes,
    q_ref,
    k_ref,
    v_ref,
    ids_ref,
    table_ref,
    out_ref,
    rows_buf,
    ids_buf,
    place_buf,
    q_slots,
    k_slots,
    v_slots,
    group_out,
    out_buf,
    sem_send,
    sem_recv,
    sem_out_send,
    sem_out_recv,
):
    dp_count, seq_count, capacity, group = sizes
    count = dp_count * seq_count
    row_count = q_ref.shape[0]
    slot_count = dp_count * capacity
    me = lax.axis_index("dp") * seq_count + lax.axis_index("seq")
    sources = (k_ref, q_ref, v_ref)

    def device_of(index):
        return (index // seq_count, index % seq_count)

    def head_columns(index):
        return pl.ds(pl.multiple_of(index * HEAD_DIM, HEAD_DIM), HEAD_DIM)

    def part_copy(part, target, origin):
        return pltpu.make_async_remote_copy(
            src_ref=sources[part].at[:, head_columns(target)],
            dst_ref=rows_buf.at[origin, :, pl.ds(part * HEAD_DIM, HEAD_DIM)],
            send_sem=sem_send.at[part, target],
            recv_sem=sem_recv.at[part, origin],
            device_id=device_of(target),
            device_id_type=pl.DeviceIdType.MESH,
        )

    def ids_copy(target, origin):
        return pltpu.make_async_remote_copy(
            src_ref=ids_ref,
            dst_ref=ids_buf.at[origin],
            send_sem=sem_send.at[3, target],
            recv_sem=sem_recv.at[3, origin],
            device_id=device_of(target),
            device_id_type=pl.DeviceIdType.MESH,
        )

    def own_copy(part):
        return pltpu.make_async_copy(
            sources[part].at[:, head_columns(me)],
            rows_buf.at[me, :, pl.ds(part * HEAD_DIM, HEAD_DIM)],
            sem_recv.at[part, me],
        )

    def out_copy(target, origin):
        return pltpu.make_async_remote_copy(
            src_ref=out_buf.at[target],
            dst_ref=out_ref.at[:, head_columns(origin)],
            send_sem=sem_out_send.at[target],
            recv_sem=sem_out_recv.at[origin],
            device_id=device_of(target),
            device_id_type=pl.DeviceIdType.MESH,
        )

    def own_out():
        return pltpu.make_async_copy(
            out_buf.at[me], out_ref.at[:, head_columns(me)], sem_out_send.at[me]
        )

    for part in range(3):
        own_copy(part).start()

    barrier = pltpu.get_barrier_semaphore()

    @pl.loop(1, count)
    def _(step):
        pl.semaphore_signal(
            barrier,
            inc=1,
            device_id=device_of((me + step) % count),
            device_id_type=pl.DeviceIdType.MESH,
        )

    pl.semaphore_wait(barrier, count - 1)

    @pl.loop(1, count)
    def _(step):
        ids_copy((me + step) % count, me).start()

    @pl.loop(1, count)
    def _(step):
        part_copy(0, (me + step) % count, me).start()
        part_copy(1, (me + step) % count, me).start()

    @pl.loop(1, count)
    def _(step):
        part_copy(2, (me + step) % count, me).start()

    v_slots[:, :, HEAD_DIM:] = jnp.ones(
        (dp_count, count * capacity, HEAD_DIM), jnp.bfloat16
    )
    before = (
        lax.broadcasted_iota(jnp.int32, (row_count, row_count), 0)
        < lax.broadcasted_iota(jnp.int32, (row_count, row_count), 1)
    ).astype(jnp.bfloat16)
    part_lane = lax.broadcasted_iota(jnp.int32, (1, HEAD_DIM), 1) < SEG_BIN

    def place_qk(origin, ids):
        ids_row = ids[0:1, :]
        bins = ids_row // SEG_BIN
        member = ids_row - bins * SEG_BIN
        bin_hits = lax.broadcasted_iota(jnp.int32, (16, row_count), 0) == bins
        ranks = jnp.dot(
            bin_hits.astype(jnp.bfloat16), before, preferred_element_type=jnp.float32
        )
        rank = jnp.sum(jnp.where(bin_hits, ranks, 0.0), axis=0, keepdims=True)
        slot = bins * capacity + rank.astype(jnp.int32)
        place = (
            lax.broadcasted_iota(jnp.int32, (slot_count, row_count), 0) == slot
        ).astype(jnp.bfloat16)
        place_buf[origin] = place
        member_hits = (
            lax.broadcasted_iota(jnp.int32, (HEAD_DIM, row_count), 0) == member
        )
        own_member = lax.dot_general(
            place, member_hits.astype(jnp.bfloat16), NT, preferred_element_type=jnp.float32
        )
        other_member = lax.dot_general(
            place,
            jnp.logical_not(member_hits).astype(jnp.bfloat16),
            NT,
            preferred_element_type=jnp.float32,
        )
        q_marks = jnp.where(part_lane, (own_member - 1.0) * EXCLUDED, 0.0)
        k_marks = jnp.where(part_lane, 1.0 - other_member, 0.0)
        placed = jnp.dot(
            place, rows_buf[origin, :, : 2 * HEAD_DIM], preferred_element_type=jnp.float32
        ).astype(jnp.bfloat16)
        at = pl.ds(pl.multiple_of(origin * capacity, capacity), capacity)
        shape = (dp_count, capacity, HEAD_DIM)
        k_slots[:, at, :HEAD_DIM] = placed[:, :HEAD_DIM].reshape(shape)
        q_slots[:, at, :HEAD_DIM] = placed[:, HEAD_DIM:].reshape(shape)
        k_slots[:, at, HEAD_DIM:] = k_marks.astype(jnp.bfloat16).reshape(shape)
        q_slots[:, at, HEAD_DIM:] = q_marks.astype(jnp.bfloat16).reshape(shape)

    def place_v(origin):
        placed = jnp.dot(
            place_buf[origin],
            rows_buf[origin, :, 2 * HEAD_DIM :],
            preferred_element_type=jnp.float32,
        ).astype(jnp.bfloat16)
        at = pl.ds(pl.multiple_of(origin * capacity, capacity), capacity)
        v_slots[:, at, :HEAD_DIM] = placed.reshape((dp_count, capacity, HEAD_DIM))

    own_copy(0).wait()
    own_copy(1).wait()
    place_qk(me, ids_ref[...])

    @pl.loop(1, count)
    def _(step):
        origin = (me - step + count) % count
        ids_copy(me, origin).wait_recv()
        part_copy(0, me, origin).wait_recv()
        part_copy(1, me, origin).wait_recv()
        place_qk(origin, ids_buf[origin])

    own_copy(2).wait()
    place_v(me)

    @pl.loop(1, count)
    def _(step):
        origin = (me - step + count) % count
        part_copy(2, me, origin).wait_recv()
        place_v(origin)

    exponent_scale = 1.0 / (math.sqrt(HEAD_DIM) * math.log(2.0))
    group_slots = group * capacity

    @pl.loop(0, count // group)
    def _(turn):
        first = ((me // group + turn + 1) % (count // group)) * group
        at = pl.ds(pl.multiple_of(first * capacity, group_slots), group_slots)

        @pl.loop(0, dp_count)
        def _(bin_index):
            query = q_slots[bin_index, at, :]
            scores = lax.dot_general(
                query, k_slots[bin_index], NT, preferred_element_type=jnp.float32
            )
            row_max = jnp.max(scores, axis=1, keepdims=True)
            weights = jnp.exp2((scores - row_max) * exponent_scale).astype(jnp.bfloat16)
            sums = jnp.dot(weights, v_slots[bin_index], preferred_element_type=jnp.float32)
            attended = (sums[:, :HEAD_DIM] / sums[:, HEAD_DIM:]).astype(jnp.bfloat16)
            factor = jnp.zeros((group_slots, HEAD_DIM), jnp.float32)
            for member in range(SEG_BIN):
                mark = query[:, HEAD_DIM + member : HEAD_DIM + member + 1].astype(jnp.float32)
                row = table_ref[pl.ds(bin_index * SEG_BIN + member, 1), :]
                factor = jnp.where(mark == 0.0, 1.0 + row, factor)
            mixed = (attended.astype(jnp.float32) * factor).astype(jnp.bfloat16)
            group_out[bin_index] = mixed

        for inner in range(group):
            target = first + inner
            slots = group_out[:, inner * capacity : (inner + 1) * capacity, :].reshape(
                (slot_count, HEAD_DIM)
            )
            out_buf[target] = lax.dot_general(
                place_buf[target], slots, TN, preferred_element_type=jnp.float32
            ).astype(jnp.bfloat16)

            @pl.when(target != me)
            def _():
                out_copy(target, me).start()

            @pl.when(target == me)
            def _():
                own_out().start()

    @pl.loop(1, count)
    def _(step):
        target = (me + step) % count
        ids_copy(target, me).wait_send()
        part_copy(0, target, me).wait_send()
        part_copy(1, target, me).wait_send()
        part_copy(2, target, me).wait_send()
        out_copy(target, me).wait_send()
        out_copy(me, target).wait_recv()

    own_out().wait()


def head_shards(query_rows, key_rows, value_rows, seg_ids, timesteps, w_mod):
    dp_count = lax.axis_size("dp")
    seq_count = lax.axis_size("seq")
    count = dp_count * seq_count
    row_count, width = query_rows.shape
    capacity = 2 * row_count // dp_count
    group = min(8, count)
    me = lax.axis_index("dp") * seq_count + lax.axis_index("seq")
    head_weights = lax.dynamic_slice_in_dim(w_mod, me * HEAD_DIM, HEAD_DIM, 1)
    scale_table = scale_rows_table(timesteps, head_weights)
    ids = jnp.broadcast_to(seg_ids[None, :], (8, row_count))
    vmem = pl.BlockSpec(memory_space=pltpu.VMEM)
    anywhere = pl.BlockSpec(memory_space=pl.ANY)
    slots = (dp_count, count * capacity, 2 * HEAD_DIM)
    return pl.pallas_call(
        functools.partial(head_kernel, (dp_count, seq_count, capacity, group)),
        out_shape=jax.ShapeDtypeStruct((row_count, width), jnp.bfloat16),
        in_specs=[anywhere, anywhere, anywhere, vmem, vmem],
        out_specs=anywhere,
        scratch_shapes=[
            pltpu.VMEM((count, row_count, 3 * HEAD_DIM), jnp.bfloat16),
            pltpu.VMEM((count, 8, row_count), jnp.int32),
            pltpu.VMEM((count, dp_count * capacity, row_count), jnp.bfloat16),
            pltpu.VMEM(slots, jnp.bfloat16),
            pltpu.VMEM(slots, jnp.bfloat16),
            pltpu.VMEM(slots, jnp.bfloat16),
            pltpu.VMEM((dp_count, group * capacity, HEAD_DIM), jnp.bfloat16),
            pltpu.VMEM((count, row_count, HEAD_DIM), jnp.bfloat16),
            pltpu.SemaphoreType.DMA((4, count)),
            pltpu.SemaphoreType.DMA((4, count)),
            pltpu.SemaphoreType.DMA((count,)),
            pltpu.SemaphoreType.DMA((count,)),
        ],
        compiler_params=pltpu.CompilerParams(
            collective_id=0, has_side_effects=True, vmem_limit_bytes=56 * 1024 * 1024
        ),
    )(query_rows, key_rows, value_rows, ids, scale_table)


def shards(query_rows, key_rows, value_rows, seg_ids, timesteps, w_mod):
    count = lax.axis_size("dp") * lax.axis_size("seq")
    whole_heads = query_rows.shape[1] == count * HEAD_DIM
    body = head_shards if whole_heads else routed_shards
    return body(query_rows, key_rows, value_rows, seg_ids, timesteps, w_mod)


def solution(mesh):
    placed = (
        P(("dp", "seq"), None),
        P(("dp", "seq"), None),
        P(("dp", "seq"), None),
        P(("dp", "seq")),
        P(),
        P(),
    )
    return jax.shard_map(
        shards, mesh=mesh, in_specs=placed, out_specs=P(("dp", "seq"), None), check_vma=False
    )
```

```python
import functools
import math

import jax
import jax.numpy as jnp
from jax import lax
from jax.experimental import pallas as pl
from jax.experimental.pallas import tpu as pltpu
from jax.sharding import PartitionSpec as P

HEAD_DIM = 128
FREQ = 256
SEG_BIN = 2


def for_sending(value):
    return jax.tree.map(lambda a: a.astype(jnp.bfloat16) if a.dtype == jnp.float32 else a, value)


def scale_rows_table(timesteps, w_mod):
    half_freq = FREQ // 2
    frequencies = jnp.exp(-math.log(10000.0) * jnp.arange(half_freq, dtype=jnp.float32) / half_freq)
    angles = timesteps.astype(jnp.float32)[:, None] * frequencies[None, :]
    embedding = jnp.concatenate([jnp.cos(angles), jnp.sin(angles)], axis=1)
    activated = jax.nn.silu(embedding).astype(jnp.bfloat16)
    return jnp.dot(activated, w_mod, preferred_element_type=jnp.float32)


def slot_places(row_bins, bin_count, capacity):
    bin_hits = (row_bins[:, None] == jnp.arange(bin_count, dtype=jnp.int32)[None, :]).astype(
        jnp.int32
    )
    ranks = jnp.cumsum(bin_hits, axis=0) - bin_hits
    slot_rank = jnp.sum(ranks * bin_hits, axis=1)
    target = row_bins * capacity + slot_rank
    return jnp.arange(bin_count * capacity, dtype=jnp.int32)[:, None] == target[None, :]


def slot_ids_of(placement, sample_ids):
    return jnp.sum(jnp.where(placement, sample_ids[None, :] + 1, 0), axis=1) - 1


def attend_slots(query_part, key_part, value_part, sample_ids):
    length, row_width = query_part.shape
    head_count = row_width // HEAD_DIM
    block_rows = min(512, length)
    score_scale = 1.0 / math.sqrt(HEAD_DIM)
    query_blocks = query_part.reshape(length // block_rows, block_rows, head_count, HEAD_DIM)
    key_heads = key_part.reshape(length, head_count, HEAD_DIM)
    value_heads = value_part.reshape(length, head_count, HEAD_DIM)
    id_blocks = sample_ids.reshape(length // block_rows, block_rows)

    def one_block(block_pair):
        query_block, query_ids = block_pair
        scores = (
            jnp.einsum("qhd,khd->hqk", query_block, key_heads, preferred_element_type=jnp.float32)
            * score_scale
        )
        same_sample = query_ids[:, None] == sample_ids[None, :]
        scores = jnp.where(same_sample[None], scores, -1e30)
        row_max = jnp.max(scores, axis=2, keepdims=True)
        weights = jnp.exp(scores - row_max)
        soft_probs = (weights / jnp.sum(weights, axis=2, keepdims=True)).astype(jnp.bfloat16)
        block_out = jnp.einsum(
            "hqk,khd->qhd", soft_probs, value_heads, preferred_element_type=jnp.float32
        )
        return block_out.astype(jnp.bfloat16).reshape(block_rows, row_width)

    return lax.map(one_block, (query_blocks, id_blocks)).reshape(length, row_width)


def place_rows(place_mask, arrays):
    return tuple(
        (
            jnp.dot(place_mask, single, preferred_element_type=jnp.float32).astype(jnp.bfloat16)
            for single in arrays
        )
    )


def routed_shards(query_rows, key_rows, value_rows, seg_ids, timesteps, w_mod):
    dp_count = lax.axis_size("dp")
    seq_count = lax.axis_size("seq")
    row_count = query_rows.shape[0]
    capacity = 2 * row_count // dp_count
    ids_tiled = jnp.broadcast_to(seg_ids[:, None], (row_count, seq_count))
    group_ids = lax.all_to_all(ids_tiled, "seq", split_axis=1, concat_axis=0, tiled=True).reshape(
        -1
    )
    head_parts = (
        lax.all_to_all(query_rows, "seq", split_axis=1, concat_axis=0, tiled=True),
        lax.all_to_all(key_rows, "seq", split_axis=1, concat_axis=0, tiled=True),
        lax.all_to_all(value_rows, "seq", split_axis=1, concat_axis=0, tiled=True),
    )
    placement = slot_places(group_ids // SEG_BIN, dp_count, seq_count * capacity)
    place_mask = placement.astype(jnp.bfloat16)
    slotted = place_rows(place_mask, head_parts)
    bin_ids = lax.all_to_all(
        slot_ids_of(placement, group_ids), "dp", split_axis=0, concat_axis=0, tiled=True
    )
    bin_query, bin_key, bin_value = jax.tree.map(
        lambda part, own: part.astype(own.dtype),
        lax.all_to_all(for_sending(slotted), "dp", split_axis=0, concat_axis=0, tiled=True),
        slotted,
    )
    attended = attend_slots(bin_query, bin_key, bin_value, bin_ids)
    returned = lax.all_to_all(attended, "dp", split_axis=0, concat_axis=0, tiled=True)
    unslotted = jnp.dot(place_mask.T, returned, preferred_element_type=jnp.float32).astype(
        jnp.bfloat16
    )
    home_rows = lax.all_to_all(unslotted, "seq", split_axis=0, concat_axis=1, tiled=True)
    scale_table = scale_rows_table(timesteps, w_mod)
    lookup = (
        seg_ids[:, None] == jnp.arange(scale_table.shape[0], dtype=jnp.int32)[None, :]
    ).astype(jnp.float32)
    row_scales = jnp.dot(
        lookup, scale_table, precision=lax.Precision.HIGHEST, preferred_element_type=jnp.float32
    )
    return (home_rows.astype(jnp.float32) * (1.0 + row_scales)).astype(jnp.bfloat16)


EXCLUDED = float(1 << 20)
NT = (((1,), (1,)), ((), ()))
TN = (((0,), (0,)), ((), ()))


def head_kernel(
    sizes,
    q_ref,
    k_ref,
    v_ref,
    ids_ref,
    table_ref,
    out_ref,
    rows_buf,
    ids_buf,
    place_buf,
    q_slots,
    k_slots,
    v_slots,
    weights_buf,
    group_out,
    out_buf,
    sem_send,
    sem_recv,
    sem_out_send,
    sem_out_recv,
):
    dp_count, seq_count, capacity, group = sizes
    count = dp_count * seq_count
    row_count = q_ref.shape[0]
    slot_count = dp_count * capacity
    me = lax.axis_index("dp") * seq_count + lax.axis_index("seq")
    sources = (k_ref, q_ref, v_ref)

    def device_of(index):
        return (index // seq_count, index % seq_count)

    half = count // 2

    def peer(away, shift):
        return ((me // half + away) % 2) * half + (me % half + shift + half) % half

    def each_peer(visit):
        @pl.loop(0, half)
        def _(shift):
            visit(1, shift)

            @pl.when(shift > 0)
            def _():
                visit(0, shift)

    def head_columns(index):
        return pl.ds(pl.multiple_of(index * HEAD_DIM, HEAD_DIM), HEAD_DIM)

    def part_copy(part, target, origin):
        return pltpu.make_async_remote_copy(
            src_ref=sources[part].at[:, head_columns(target)],
            dst_ref=rows_buf.at[origin, :, pl.ds(part * HEAD_DIM, HEAD_DIM)],
            send_sem=sem_send.at[part, target],
            recv_sem=sem_recv.at[part, origin],
            device_id=device_of(target),
            device_id_type=pl.DeviceIdType.MESH,
        )

    def ids_copy(target, origin):
        return pltpu.make_async_remote_copy(
            src_ref=ids_ref,
            dst_ref=ids_buf.at[origin],
            send_sem=sem_send.at[3, target],
            recv_sem=sem_recv.at[3, origin],
            device_id=device_of(target),
            device_id_type=pl.DeviceIdType.MESH,
        )

    def own_copy(part):
        return pltpu.make_async_copy(
            sources[part].at[:, head_columns(me)],
            rows_buf.at[me, :, pl.ds(part * HEAD_DIM, HEAD_DIM)],
            sem_recv.at[part, me],
        )

    def out_copy(target, origin):
        return pltpu.make_async_remote_copy(
            src_ref=out_buf.at[target],
            dst_ref=out_ref.at[:, head_columns(origin)],
            send_sem=sem_out_send.at[target],
            recv_sem=sem_out_recv.at[origin],
            device_id=device_of(target),
            device_id_type=pl.DeviceIdType.MESH,
        )

    def own_out():
        return pltpu.make_async_copy(
            out_buf.at[me], out_ref.at[:, head_columns(me)], sem_out_send.at[me]
        )

    for part in range(3):
        own_copy(part).start()

    barrier = pltpu.get_barrier_semaphore()

    def greet(away, shift):
        pl.semaphore_signal(
            barrier,
            inc=1,
            device_id=device_of(peer(away, shift)),
            device_id_type=pl.DeviceIdType.MESH,
        )

    each_peer(greet)
    pl.semaphore_wait(barrier, count - 1)

    def send_qk(away, shift):
        target = peer(away, shift)
        ids_copy(target, me).start()
        part_copy(0, target, me).start()
        part_copy(1, target, me).start()

    each_peer(send_qk)
    each_peer(lambda away, shift: part_copy(2, peer(away, shift), me).start())

    v_slots[:, :, HEAD_DIM:] = jnp.ones(
        (dp_count, count * capacity, HEAD_DIM), jnp.bfloat16
    )
    before = (
        lax.broadcasted_iota(jnp.int32, (row_count, row_count), 0)
        < lax.broadcasted_iota(jnp.int32, (row_count, row_count), 1)
    ).astype(jnp.bfloat16)
    part_lane = lax.broadcasted_iota(jnp.int32, (1, HEAD_DIM), 1) < SEG_BIN

    def place_qk(origin, ids):
        bins = ids // SEG_BIN
        member = ids - bins * SEG_BIN
        bin_hits = lax.broadcasted_iota(jnp.int32, (16, row_count), 0) == bins
        ranks = jnp.dot(
            bin_hits.astype(jnp.bfloat16), before, preferred_element_type=jnp.float32
        )
        rank = jnp.sum(jnp.where(bin_hits, ranks, 0.0), axis=0, keepdims=True)
        slot = bins * capacity + rank.astype(jnp.int32)
        place = (
            lax.broadcasted_iota(jnp.int32, (slot_count, row_count), 0) == slot
        ).astype(jnp.bfloat16)
        place_buf[origin] = place
        member_hits = (
            lax.broadcasted_iota(jnp.int32, (HEAD_DIM, row_count), 0) == member
        )
        own_member = lax.dot_general(
            place, member_hits.astype(jnp.bfloat16), NT, preferred_element_type=jnp.float32
        )
        other_member = lax.dot_general(
            place,
            jnp.logical_not(member_hits).astype(jnp.bfloat16),
            NT,
            preferred_element_type=jnp.float32,
        )
        q_marks = jnp.where(part_lane, (own_member - 1.0) * EXCLUDED, 0.0)
        k_marks = jnp.where(part_lane, 1.0 - other_member, 0.0)
        placed = jnp.dot(
            place, rows_buf[origin, :, : 2 * HEAD_DIM], preferred_element_type=jnp.float32
        ).astype(jnp.bfloat16)
        at = pl.ds(pl.multiple_of(origin * capacity, capacity), capacity)
        shape = (dp_count, capacity, HEAD_DIM)
        k_slots[:, at, :HEAD_DIM] = placed[:, :HEAD_DIM].reshape(shape)
        q_slots[:, at, :HEAD_DIM] = placed[:, HEAD_DIM:].reshape(shape)
        k_slots[:, at, HEAD_DIM:] = k_marks.astype(jnp.bfloat16).reshape(shape)
        q_slots[:, at, HEAD_DIM:] = q_marks.astype(jnp.bfloat16).reshape(shape)

    def place_v(origin):
        placed = jnp.dot(
            place_buf[origin],
            rows_buf[origin, :, 2 * HEAD_DIM :],
            preferred_element_type=jnp.float32,
        ).astype(jnp.bfloat16)
        at = pl.ds(pl.multiple_of(origin * capacity, capacity), capacity)
        v_slots[:, at, :HEAD_DIM] = placed.reshape((dp_count, capacity, HEAD_DIM))

    own_copy(0).wait()
    own_copy(1).wait()
    place_qk(me, ids_ref[...])

    def take_qk(away, shift):
        origin = peer(away, -shift)
        ids_copy(me, origin).wait_recv()
        part_copy(0, me, origin).wait_recv()
        part_copy(1, me, origin).wait_recv()
        place_qk(origin, ids_buf[origin])

    each_peer(take_qk)

    exponent_scale = 1.0 / (math.sqrt(HEAD_DIM) * math.log(2.0))
    group_slots = group * capacity
    groups = count // group

    def group_at(turn):
        first = ((me // group + groups // 2 + turn) % groups) * group
        return first, pl.ds(pl.multiple_of(first * capacity, group_slots), group_slots)

    @pl.loop(0, groups)
    def _(turn):
        _, at = group_at(turn)

        @pl.loop(0, dp_count)
        def _(bin_index):
            scores = lax.dot_general(
                q_slots[bin_index, at, :],
                k_slots[bin_index],
                NT,
                preferred_element_type=jnp.float32,
            )
            row_max = jnp.max(scores, axis=1, keepdims=True)
            weights_buf[bin_index, at, :] = jnp.exp2(
                (scores - row_max) * exponent_scale
            ).astype(jnp.bfloat16)

    own_copy(2).wait()
    place_v(me)

    @pl.loop(1, half)
    def _(shift):
        origin = peer(0, -shift)
        part_copy(2, me, origin).wait_recv()
        place_v(origin)

    @pl.loop(0, half)
    def _(shift):
        origin = peer(1, -shift)
        part_copy(2, me, origin).wait_recv()
        place_v(origin)

    @pl.loop(0, groups)
    def _(turn):
        first, at = group_at(turn)

        @pl.loop(0, dp_count)
        def _(bin_index):
            query_marks = q_slots[bin_index, at, HEAD_DIM:]
            sums = jnp.dot(
                weights_buf[bin_index, at, :],
                v_slots[bin_index],
                preferred_element_type=jnp.float32,
            )
            attended = (sums[:, :HEAD_DIM] / sums[:, HEAD_DIM:]).astype(jnp.bfloat16)
            factor = jnp.zeros((group_slots, HEAD_DIM), jnp.float32)
            for member in range(SEG_BIN):
                mark = query_marks[:, member : member + 1].astype(jnp.float32)
                row = table_ref[pl.ds(bin_index * SEG_BIN + member, 1), :]
                factor = jnp.where(mark == 0.0, 1.0 + row, factor)
            mixed = (attended.astype(jnp.float32) * factor).astype(jnp.bfloat16)
            group_out[bin_index] = mixed

        for inner in range(group):
            target = first + inner
            slots = group_out[:, inner * capacity : (inner + 1) * capacity, :].reshape(
                (slot_count, HEAD_DIM)
            )
            out_buf[target] = lax.dot_general(
                place_buf[target], slots, TN, preferred_element_type=jnp.float32
            ).astype(jnp.bfloat16)

            @pl.when(target != me)
            def _():
                out_copy(target, me).start()

            @pl.when(target == me)
            def _():
                own_out().start()

    @pl.loop(1, count)
    def _(step):
        target = (me + step) % count
        ids_copy(target, me).wait_send()
        part_copy(0, target, me).wait_send()
        part_copy(1, target, me).wait_send()
        part_copy(2, target, me).wait_send()
        out_copy(target, me).wait_send()
        out_copy(me, target).wait_recv()

    own_out().wait()


def head_shards(query_rows, key_rows, value_rows, seg_ids, timesteps, w_mod):
    dp_count = lax.axis_size("dp")
    seq_count = lax.axis_size("seq")
    count = dp_count * seq_count
    row_count, width = query_rows.shape
    capacity = 2 * row_count // dp_count
    group = count // 4
    me = lax.axis_index("dp") * seq_count + lax.axis_index("seq")
    head_weights = lax.dynamic_slice_in_dim(w_mod, me * HEAD_DIM, HEAD_DIM, 1)
    scale_table = scale_rows_table(timesteps, head_weights)
    ids = seg_ids.reshape(1, row_count)
    vmem = pl.BlockSpec(memory_space=pltpu.VMEM)
    anywhere = pl.BlockSpec(memory_space=pl.ANY)
    slots = (dp_count, count * capacity, 2 * HEAD_DIM)
    return pl.pallas_call(
        functools.partial(head_kernel, (dp_count, seq_count, capacity, group)),
        out_shape=jax.ShapeDtypeStruct((row_count, width), jnp.bfloat16),
        in_specs=[anywhere, anywhere, anywhere, vmem, vmem],
        out_specs=anywhere,
        scratch_shapes=[
            pltpu.VMEM((count, row_count, 3 * HEAD_DIM), jnp.bfloat16),
            pltpu.VMEM((count, 1, row_count), jnp.int32),
            pltpu.VMEM((count, dp_count * capacity, row_count), jnp.bfloat16),
            pltpu.VMEM(slots, jnp.bfloat16),
            pltpu.VMEM(slots, jnp.bfloat16),
            pltpu.VMEM(slots, jnp.bfloat16),
            pltpu.VMEM((dp_count, count * capacity, count * capacity), jnp.bfloat16),
            pltpu.VMEM((dp_count, group * capacity, HEAD_DIM), jnp.bfloat16),
            pltpu.VMEM((count, row_count, HEAD_DIM), jnp.bfloat16),
            pltpu.SemaphoreType.DMA((4, count)),
            pltpu.SemaphoreType.DMA((4, count)),
            pltpu.SemaphoreType.DMA((count,)),
            pltpu.SemaphoreType.DMA((count,)),
        ],
        compiler_params=pltpu.CompilerParams(
            collective_id=0, has_side_effects=True, vmem_limit_bytes=56 * 1024 * 1024
        ),
    )(query_rows, key_rows, value_rows, ids, scale_table)


def shards(query_rows, key_rows, value_rows, seg_ids, timesteps, w_mod):
    count = lax.axis_size("dp") * lax.axis_size("seq")
    whole_heads = query_rows.shape[1] == count * HEAD_DIM
    body = head_shards if whole_heads else routed_shards
    return body(query_rows, key_rows, value_rows, seg_ids, timesteps, w_mod)


def solution(mesh):
    placed = (
        P(("dp", "seq"), None),
        P(("dp", "seq"), None),
        P(("dp", "seq"), None),
        P(("dp", "seq")),
        P(),
        P(),
    )
    return jax.shard_map(
        shards, mesh=mesh, in_specs=placed, out_specs=P(("dp", "seq"), None), check_vma=False
    )
```

```python
import functools
import math

import jax
import jax.numpy as jnp
from jax import lax
from jax.experimental import pallas as pl
from jax.experimental.pallas import tpu as pltpu
from jax.sharding import PartitionSpec as P

HEAD_DIM = 128
FREQ = 256
SEG_BIN = 2


def for_sending(value):
    return jax.tree.map(lambda a: a.astype(jnp.bfloat16) if a.dtype == jnp.float32 else a, value)


def scale_rows_table(timesteps, w_mod):
    half_freq = FREQ // 2
    frequencies = jnp.exp(-math.log(10000.0) * jnp.arange(half_freq, dtype=jnp.float32) / half_freq)
    angles = timesteps.astype(jnp.float32)[:, None] * frequencies[None, :]
    embedding = jnp.concatenate([jnp.cos(angles), jnp.sin(angles)], axis=1)
    activated = jax.nn.silu(embedding).astype(jnp.bfloat16)
    return jnp.dot(activated, w_mod, preferred_element_type=jnp.float32)


def slot_places(row_bins, bin_count, capacity):
    bin_hits = (row_bins[:, None] == jnp.arange(bin_count, dtype=jnp.int32)[None, :]).astype(
        jnp.int32
    )
    ranks = jnp.cumsum(bin_hits, axis=0) - bin_hits
    slot_rank = jnp.sum(ranks * bin_hits, axis=1)
    target = row_bins * capacity + slot_rank
    return jnp.arange(bin_count * capacity, dtype=jnp.int32)[:, None] == target[None, :]


def slot_ids_of(placement, sample_ids):
    return jnp.sum(jnp.where(placement, sample_ids[None, :] + 1, 0), axis=1) - 1


def attend_slots(query_part, key_part, value_part, sample_ids):
    length, row_width = query_part.shape
    head_count = row_width // HEAD_DIM
    block_rows = min(512, length)
    score_scale = 1.0 / math.sqrt(HEAD_DIM)
    query_blocks = query_part.reshape(length // block_rows, block_rows, head_count, HEAD_DIM)
    key_heads = key_part.reshape(length, head_count, HEAD_DIM)
    value_heads = value_part.reshape(length, head_count, HEAD_DIM)
    id_blocks = sample_ids.reshape(length // block_rows, block_rows)

    def one_block(block_pair):
        query_block, query_ids = block_pair
        scores = (
            jnp.einsum("qhd,khd->hqk", query_block, key_heads, preferred_element_type=jnp.float32)
            * score_scale
        )
        same_sample = query_ids[:, None] == sample_ids[None, :]
        scores = jnp.where(same_sample[None], scores, -1e30)
        row_max = jnp.max(scores, axis=2, keepdims=True)
        weights = jnp.exp(scores - row_max)
        soft_probs = (weights / jnp.sum(weights, axis=2, keepdims=True)).astype(jnp.bfloat16)
        block_out = jnp.einsum(
            "hqk,khd->qhd", soft_probs, value_heads, preferred_element_type=jnp.float32
        )
        return block_out.astype(jnp.bfloat16).reshape(block_rows, row_width)

    return lax.map(one_block, (query_blocks, id_blocks)).reshape(length, row_width)


def place_rows(place_mask, arrays):
    return tuple(
        (
            jnp.dot(place_mask, single, preferred_element_type=jnp.float32).astype(jnp.bfloat16)
            for single in arrays
        )
    )


def routed_shards(query_rows, key_rows, value_rows, seg_ids, timesteps, w_mod):
    dp_count = lax.axis_size("dp")
    seq_count = lax.axis_size("seq")
    row_count = query_rows.shape[0]
    capacity = 2 * row_count // dp_count
    ids_tiled = jnp.broadcast_to(seg_ids[:, None], (row_count, seq_count))
    group_ids = lax.all_to_all(ids_tiled, "seq", split_axis=1, concat_axis=0, tiled=True).reshape(
        -1
    )
    head_parts = (
        lax.all_to_all(query_rows, "seq", split_axis=1, concat_axis=0, tiled=True),
        lax.all_to_all(key_rows, "seq", split_axis=1, concat_axis=0, tiled=True),
        lax.all_to_all(value_rows, "seq", split_axis=1, concat_axis=0, tiled=True),
    )
    placement = slot_places(group_ids // SEG_BIN, dp_count, seq_count * capacity)
    place_mask = placement.astype(jnp.bfloat16)
    slotted = place_rows(place_mask, head_parts)
    bin_ids = lax.all_to_all(
        slot_ids_of(placement, group_ids), "dp", split_axis=0, concat_axis=0, tiled=True
    )
    bin_query, bin_key, bin_value = jax.tree.map(
        lambda part, own: part.astype(own.dtype),
        lax.all_to_all(for_sending(slotted), "dp", split_axis=0, concat_axis=0, tiled=True),
        slotted,
    )
    attended = attend_slots(bin_query, bin_key, bin_value, bin_ids)
    returned = lax.all_to_all(attended, "dp", split_axis=0, concat_axis=0, tiled=True)
    unslotted = jnp.dot(place_mask.T, returned, preferred_element_type=jnp.float32).astype(
        jnp.bfloat16
    )
    home_rows = lax.all_to_all(unslotted, "seq", split_axis=0, concat_axis=1, tiled=True)
    scale_table = scale_rows_table(timesteps, w_mod)
    lookup = (
        seg_ids[:, None] == jnp.arange(scale_table.shape[0], dtype=jnp.int32)[None, :]
    ).astype(jnp.float32)
    row_scales = jnp.dot(
        lookup, scale_table, precision=lax.Precision.HIGHEST, preferred_element_type=jnp.float32
    )
    return (home_rows.astype(jnp.float32) * (1.0 + row_scales)).astype(jnp.bfloat16)


EXCLUDED = float(1 << 20)
NT = (((1,), (1,)), ((), ()))
TN = (((0,), (0,)), ((), ()))


def head_kernel(
    sizes,
    q_ref,
    k_ref,
    v_ref,
    ids_ref,
    table_ref,
    out_ref,
    rows_buf,
    ids_buf,
    place_buf,
    q_slots,
    k_slots,
    v_slots,
    group_out,
    out_buf,
    sem_send,
    sem_recv,
    sem_out_send,
    sem_out_recv,
):
    dp_count, seq_count, capacity, group = sizes
    count = dp_count * seq_count
    row_count = q_ref.shape[0]
    slot_count = dp_count * capacity
    me = lax.axis_index("dp") * seq_count + lax.axis_index("seq")
    sources = (k_ref, v_ref, q_ref)

    def device_of(index):
        return (index // seq_count, index % seq_count)

    half = count // 2

    def peer(away, shift):
        return ((me // half + away) % 2) * half + (me % half + shift + half) % half

    def each_peer(visit):
        @pl.loop(0, half)
        def _(shift):
            visit(1, shift)

            @pl.when(shift > 0)
            def _():
                visit(0, shift)

    def head_columns(index):
        return pl.ds(pl.multiple_of(index * HEAD_DIM, HEAD_DIM), HEAD_DIM)

    def part_copy(part, target, origin):
        return pltpu.make_async_remote_copy(
            src_ref=sources[part].at[:, head_columns(target)],
            dst_ref=rows_buf.at[origin, :, pl.ds(part * HEAD_DIM, HEAD_DIM)],
            send_sem=sem_send.at[part, target],
            recv_sem=sem_recv.at[part, origin],
            device_id=device_of(target),
            device_id_type=pl.DeviceIdType.MESH,
        )

    def ids_copy(target, origin):
        return pltpu.make_async_remote_copy(
            src_ref=ids_ref,
            dst_ref=ids_buf.at[origin],
            send_sem=sem_send.at[3, target],
            recv_sem=sem_recv.at[3, origin],
            device_id=device_of(target),
            device_id_type=pl.DeviceIdType.MESH,
        )

    def own_copy(part):
        return pltpu.make_async_copy(
            sources[part].at[:, head_columns(me)],
            rows_buf.at[me, :, pl.ds(part * HEAD_DIM, HEAD_DIM)],
            sem_recv.at[part, me],
        )

    def out_copy(target, origin):
        return pltpu.make_async_remote_copy(
            src_ref=out_buf.at[target],
            dst_ref=out_ref.at[:, head_columns(origin)],
            send_sem=sem_out_send.at[target],
            recv_sem=sem_out_recv.at[origin],
            device_id=device_of(target),
            device_id_type=pl.DeviceIdType.MESH,
        )

    def own_out():
        return pltpu.make_async_copy(
            out_buf.at[me], out_ref.at[:, head_columns(me)], sem_out_send.at[me]
        )

    for part in range(3):
        own_copy(part).start()

    barrier = pltpu.get_barrier_semaphore()

    def greet(away, shift):
        pl.semaphore_signal(
            barrier,
            inc=1,
            device_id=device_of(peer(away, shift)),
            device_id_type=pl.DeviceIdType.MESH,
        )

    each_peer(greet)
    pl.semaphore_wait(barrier, count - 1)

    def send_first(away, shift):
        target = peer(away, shift)
        ids_copy(target, me).start()
        part_copy(0, target, me).start()

    each_peer(send_first)
    for part in (1, 2):
        each_peer(lambda away, shift: part_copy(part, peer(away, shift), me).start())

    v_slots[:, :, HEAD_DIM:] = jnp.ones(
        (dp_count, count * capacity, HEAD_DIM), jnp.bfloat16
    )
    before = (
        lax.broadcasted_iota(jnp.int32, (row_count, row_count), 0)
        < lax.broadcasted_iota(jnp.int32, (row_count, row_count), 1)
    ).astype(jnp.bfloat16)
    part_lane = lax.broadcasted_iota(jnp.int32, (1, HEAD_DIM), 1) < SEG_BIN

    def member_hits(origin):
        ids = ids_buf[origin]
        member = ids - ids // SEG_BIN * SEG_BIN
        return lax.broadcasted_iota(jnp.int32, (HEAD_DIM, row_count), 0) == member

    def marks_of(place, hits):
        return lax.dot_general(
            place, hits.astype(jnp.bfloat16), NT, preferred_element_type=jnp.float32
        )

    def placed_part(place, origin, part):
        rows = rows_buf[origin, :, part * HEAD_DIM : (part + 1) * HEAD_DIM]
        return jnp.dot(place, rows, preferred_element_type=jnp.float32)

    def by_bin(value):
        return value.astype(jnp.bfloat16).reshape((dp_count, capacity, HEAD_DIM))

    def slots_at(index):
        return pl.ds(pl.multiple_of(index * capacity, capacity), capacity)

    def place_k(origin):
        bins = ids_buf[origin] // SEG_BIN
        bin_hits = lax.broadcasted_iota(jnp.int32, (16, row_count), 0) == bins
        ranks = jnp.dot(
            bin_hits.astype(jnp.bfloat16), before, preferred_element_type=jnp.float32
        )
        rank = jnp.sum(jnp.where(bin_hits, ranks, 0.0), axis=0, keepdims=True)
        slot = bins * capacity + rank.astype(jnp.int32)
        place = (
            lax.broadcasted_iota(jnp.int32, (slot_count, row_count), 0) == slot
        ).astype(jnp.bfloat16)
        place_buf[origin] = place
        other_member = marks_of(place, jnp.logical_not(member_hits(origin)))
        k_marks = jnp.where(part_lane, 1.0 - other_member, 0.0)
        k_slots[:, slots_at(origin), :HEAD_DIM] = by_bin(placed_part(place, origin, 0))
        k_slots[:, slots_at(origin), HEAD_DIM:] = by_bin(k_marks)

    def place_v(origin):
        placed = placed_part(place_buf[origin], origin, 1)
        v_slots[:, slots_at(origin), :HEAD_DIM] = by_bin(placed)

    def place_q(origin, inner):
        place = place_buf[origin]
        own_member = marks_of(place, member_hits(origin))
        q_marks = jnp.where(part_lane, (own_member - 1.0) * EXCLUDED, 0.0)
        at = slice(inner * capacity, (inner + 1) * capacity)
        q_slots[:, at, :HEAD_DIM] = by_bin(placed_part(place, origin, 2))
        q_slots[:, at, HEAD_DIM:] = by_bin(q_marks)

    ids_buf[me] = ids_ref[...]
    own_copy(0).wait()
    place_k(me)

    def take_k(away, shift):
        origin = peer(away, -shift)
        ids_copy(me, origin).wait_recv()
        part_copy(0, me, origin).wait_recv()
        place_k(origin)

    each_peer(take_k)
    own_copy(1).wait()
    place_v(me)

    def take_v(away, shift):
        origin = peer(away, -shift)
        part_copy(1, me, origin).wait_recv()
        place_v(origin)

    each_peer(take_v)

    exponent_scale = 1.0 / (math.sqrt(HEAD_DIM) * math.log(2.0))
    group_slots = group * capacity

    def attend_group(away, turn):
        for inner in range(group):
            shift = turn * group + inner
            origin = peer(away, -shift)
            if away == 0 and inner == 0:

                @pl.when(turn == 0)
                def _():
                    own_copy(2).wait()

                @pl.when(turn > 0)
                def _():
                    part_copy(2, me, origin).wait_recv()
            else:
                part_copy(2, me, origin).wait_recv()
            place_q(origin, inner)

        @pl.loop(0, dp_count, unroll=8)
        def _(bin_index):
            query = q_slots[bin_index]
            scores = lax.dot_general(
                query, k_slots[bin_index], NT, preferred_element_type=jnp.float32
            )
            row_max = jnp.max(scores, axis=1, keepdims=True)
            weights = jnp.exp2((scores - row_max) * exponent_scale).astype(jnp.bfloat16)
            sums = jnp.dot(weights, v_slots[bin_index], preferred_element_type=jnp.float32)
            attended = (sums[:, :HEAD_DIM] / sums[:, HEAD_DIM:]).astype(jnp.bfloat16)
            factor = jnp.zeros((group_slots, HEAD_DIM), jnp.float32)
            for member in range(SEG_BIN):
                mark = query[:, HEAD_DIM + member : HEAD_DIM + member + 1].astype(jnp.float32)
                row = table_ref[pl.ds(bin_index * SEG_BIN + member, 1), :]
                factor = jnp.where(mark == 0.0, 1.0 + row, factor)
            mixed = (attended.astype(jnp.float32) * factor).astype(jnp.bfloat16)
            group_out[bin_index] = mixed

        for inner in range(group):
            target = peer(away, -(turn * group + inner))
            slots = group_out[:, inner * capacity : (inner + 1) * capacity, :].reshape(
                (slot_count, HEAD_DIM)
            )
            out_buf[target] = lax.dot_general(
                place_buf[target], slots, TN, preferred_element_type=jnp.float32
            ).astype(jnp.bfloat16)
            if away == 0 and inner == 0:

                @pl.when(turn == 0)
                def _():
                    own_out().start()

                @pl.when(turn > 0)
                def _():
                    out_copy(target, me).start()
            else:
                out_copy(target, me).start()

    @pl.loop(0, half // group)
    def _(turn):
        attend_group(0, turn)
        attend_group(1, turn)

    @pl.loop(1, count)
    def _(step):
        target = (me + step) % count
        ids_copy(target, me).wait_send()
        part_copy(0, target, me).wait_send()
        part_copy(1, target, me).wait_send()
        part_copy(2, target, me).wait_send()
        out_copy(target, me).wait_send()
        out_copy(me, target).wait_recv()

    own_out().wait()


def head_shards(query_rows, key_rows, value_rows, seg_ids, timesteps, w_mod):
    dp_count = lax.axis_size("dp")
    seq_count = lax.axis_size("seq")
    count = dp_count * seq_count
    row_count, width = query_rows.shape
    capacity = 2 * row_count // dp_count
    group = count // 4
    me = lax.axis_index("dp") * seq_count + lax.axis_index("seq")
    head_weights = lax.dynamic_slice_in_dim(w_mod, me * HEAD_DIM, HEAD_DIM, 1)
    scale_table = scale_rows_table(timesteps, head_weights)
    ids = seg_ids.reshape(1, row_count)
    vmem = pl.BlockSpec(memory_space=pltpu.VMEM)
    anywhere = pl.BlockSpec(memory_space=pl.ANY)
    slots = (dp_count, count * capacity, 2 * HEAD_DIM)
    return pl.pallas_call(
        functools.partial(head_kernel, (dp_count, seq_count, capacity, group)),
        out_shape=jax.ShapeDtypeStruct((row_count, width), jnp.bfloat16),
        in_specs=[anywhere, anywhere, anywhere, vmem, vmem],
        out_specs=anywhere,
        scratch_shapes=[
            pltpu.VMEM((count, row_count, 3 * HEAD_DIM), jnp.bfloat16),
            pltpu.VMEM((count, 1, row_count), jnp.int32),
            pltpu.VMEM((count, dp_count * capacity, row_count), jnp.bfloat16),
            pltpu.VMEM((dp_count, group * capacity, 2 * HEAD_DIM), jnp.bfloat16),
            pltpu.VMEM(slots, jnp.bfloat16),
            pltpu.VMEM(slots, jnp.bfloat16),
            pltpu.VMEM((dp_count, group * capacity, HEAD_DIM), jnp.bfloat16),
            pltpu.VMEM((count, row_count, HEAD_DIM), jnp.bfloat16),
            pltpu.SemaphoreType.DMA((4, count)),
            pltpu.SemaphoreType.DMA((4, count)),
            pltpu.SemaphoreType.DMA((count,)),
            pltpu.SemaphoreType.DMA((count,)),
        ],
        compiler_params=pltpu.CompilerParams(
            collective_id=0, has_side_effects=True, vmem_limit_bytes=56 * 1024 * 1024
        ),
    )(query_rows, key_rows, value_rows, ids, scale_table)


def shards(query_rows, key_rows, value_rows, seg_ids, timesteps, w_mod):
    count = lax.axis_size("dp") * lax.axis_size("seq")
    whole_heads = query_rows.shape[1] == count * HEAD_DIM
    body = head_shards if whole_heads else routed_shards
    return body(query_rows, key_rows, value_rows, seg_ids, timesteps, w_mod)


def solution(mesh):
    placed = (
        P(("dp", "seq"), None),
        P(("dp", "seq"), None),
        P(("dp", "seq"), None),
        P(("dp", "seq")),
        P(),
        P(),
    )
    return jax.shard_map(
        shards, mesh=mesh, in_specs=placed, out_specs=P(("dp", "seq"), None), check_vma=False
    )
```

```python
import functools
import math

import jax
import jax.numpy as jnp
from jax import lax
from jax.experimental import pallas as pl
from jax.experimental.pallas import tpu as pltpu
from jax.sharding import PartitionSpec as P

HEAD_DIM = 128
FREQ = 256
SEG_BIN = 2


def for_sending(value):
    return jax.tree.map(lambda a: a.astype(jnp.bfloat16) if a.dtype == jnp.float32 else a, value)


def scale_rows_table(timesteps, w_mod):
    half_freq = FREQ // 2
    frequencies = jnp.exp(-math.log(10000.0) * jnp.arange(half_freq, dtype=jnp.float32) / half_freq)
    angles = timesteps.astype(jnp.float32)[:, None] * frequencies[None, :]
    embedding = jnp.concatenate([jnp.cos(angles), jnp.sin(angles)], axis=1)
    activated = jax.nn.silu(embedding).astype(jnp.bfloat16)
    return jnp.dot(activated, w_mod, preferred_element_type=jnp.float32)


def slot_places(row_bins, bin_count, capacity):
    bin_hits = (row_bins[:, None] == jnp.arange(bin_count, dtype=jnp.int32)[None, :]).astype(
        jnp.int32
    )
    ranks = jnp.cumsum(bin_hits, axis=0) - bin_hits
    slot_rank = jnp.sum(ranks * bin_hits, axis=1)
    target = row_bins * capacity + slot_rank
    return jnp.arange(bin_count * capacity, dtype=jnp.int32)[:, None] == target[None, :]


def slot_ids_of(placement, sample_ids):
    return jnp.sum(jnp.where(placement, sample_ids[None, :] + 1, 0), axis=1) - 1


def attend_slots(query_part, key_part, value_part, sample_ids):
    length, row_width = query_part.shape
    head_count = row_width // HEAD_DIM
    block_rows = min(512, length)
    score_scale = 1.0 / math.sqrt(HEAD_DIM)
    query_blocks = query_part.reshape(length // block_rows, block_rows, head_count, HEAD_DIM)
    key_heads = key_part.reshape(length, head_count, HEAD_DIM)
    value_heads = value_part.reshape(length, head_count, HEAD_DIM)
    id_blocks = sample_ids.reshape(length // block_rows, block_rows)

    def one_block(block_pair):
        query_block, query_ids = block_pair
        scores = (
            jnp.einsum("qhd,khd->hqk", query_block, key_heads, preferred_element_type=jnp.float32)
            * score_scale
        )
        same_sample = query_ids[:, None] == sample_ids[None, :]
        scores = jnp.where(same_sample[None], scores, -1e30)
        row_max = jnp.max(scores, axis=2, keepdims=True)
        weights = jnp.exp(scores - row_max)
        soft_probs = (weights / jnp.sum(weights, axis=2, keepdims=True)).astype(jnp.bfloat16)
        block_out = jnp.einsum(
            "hqk,khd->qhd", soft_probs, value_heads, preferred_element_type=jnp.float32
        )
        return block_out.astype(jnp.bfloat16).reshape(block_rows, row_width)

    return lax.map(one_block, (query_blocks, id_blocks)).reshape(length, row_width)


def place_rows(place_mask, arrays):
    return tuple(
        (
            jnp.dot(place_mask, single, preferred_element_type=jnp.float32).astype(jnp.bfloat16)
            for single in arrays
        )
    )


def routed_shards(query_rows, key_rows, value_rows, seg_ids, timesteps, w_mod):
    dp_count = lax.axis_size("dp")
    seq_count = lax.axis_size("seq")
    row_count = query_rows.shape[0]
    capacity = 2 * row_count // dp_count
    ids_tiled = jnp.broadcast_to(seg_ids[:, None], (row_count, seq_count))
    group_ids = lax.all_to_all(ids_tiled, "seq", split_axis=1, concat_axis=0, tiled=True).reshape(
        -1
    )
    head_parts = (
        lax.all_to_all(query_rows, "seq", split_axis=1, concat_axis=0, tiled=True),
        lax.all_to_all(key_rows, "seq", split_axis=1, concat_axis=0, tiled=True),
        lax.all_to_all(value_rows, "seq", split_axis=1, concat_axis=0, tiled=True),
    )
    placement = slot_places(group_ids // SEG_BIN, dp_count, seq_count * capacity)
    place_mask = placement.astype(jnp.bfloat16)
    slotted = place_rows(place_mask, head_parts)
    bin_ids = lax.all_to_all(
        slot_ids_of(placement, group_ids), "dp", split_axis=0, concat_axis=0, tiled=True
    )
    bin_query, bin_key, bin_value = jax.tree.map(
        lambda part, own: part.astype(own.dtype),
        lax.all_to_all(for_sending(slotted), "dp", split_axis=0, concat_axis=0, tiled=True),
        slotted,
    )
    attended = attend_slots(bin_query, bin_key, bin_value, bin_ids)
    returned = lax.all_to_all(attended, "dp", split_axis=0, concat_axis=0, tiled=True)
    unslotted = jnp.dot(place_mask.T, returned, preferred_element_type=jnp.float32).astype(
        jnp.bfloat16
    )
    home_rows = lax.all_to_all(unslotted, "seq", split_axis=0, concat_axis=1, tiled=True)
    scale_table = scale_rows_table(timesteps, w_mod)
    lookup = (
        seg_ids[:, None] == jnp.arange(scale_table.shape[0], dtype=jnp.int32)[None, :]
    ).astype(jnp.float32)
    row_scales = jnp.dot(
        lookup, scale_table, precision=lax.Precision.HIGHEST, preferred_element_type=jnp.float32
    )
    return (home_rows.astype(jnp.float32) * (1.0 + row_scales)).astype(jnp.bfloat16)


EXCLUDED = float(1 << 20)
NT = (((1,), (1,)), ((), ()))
TN = (((0,), (0,)), ((), ()))


def head_kernel(
    sizes,
    q_ref,
    k_ref,
    v_ref,
    ids_ref,
    table_ref,
    out_ref,
    rows_buf,
    ids_buf,
    place_buf,
    q_slots,
    k_slots,
    v_slots,
    group_out,
    out_buf,
    sem_send,
    sem_recv,
    sem_out_send,
    sem_out_recv,
):
    dp_count, seq_count, capacity, group = sizes
    count = dp_count * seq_count
    row_count = q_ref.shape[0]
    slot_count = dp_count * capacity
    me = lax.axis_index("dp") * seq_count + lax.axis_index("seq")
    sources = (k_ref, v_ref, q_ref)

    def device_of(index):
        return (index // seq_count, index % seq_count)

    half = count // 2

    def peer(away, shift):
        return ((me // half + away) % 2) * half + (me % half + shift + half) % half

    def each_peer(visit):
        @pl.loop(0, half)
        def _(shift):
            visit(1, shift)

            @pl.when(shift > 0)
            def _():
                visit(0, shift)

    def head_columns(index):
        return pl.ds(pl.multiple_of(index * HEAD_DIM, HEAD_DIM), HEAD_DIM)

    def part_copy(part, target, origin):
        return pltpu.make_async_remote_copy(
            src_ref=sources[part].at[:, head_columns(target)],
            dst_ref=rows_buf.at[origin, :, pl.ds(part * HEAD_DIM, HEAD_DIM)],
            send_sem=sem_send.at[part, target],
            recv_sem=sem_recv.at[part, origin],
            device_id=device_of(target),
            device_id_type=pl.DeviceIdType.MESH,
        )

    def ids_copy(target, origin):
        return pltpu.make_async_remote_copy(
            src_ref=ids_ref,
            dst_ref=ids_buf.at[origin],
            send_sem=sem_send.at[3, target],
            recv_sem=sem_recv.at[3, origin],
            device_id=device_of(target),
            device_id_type=pl.DeviceIdType.MESH,
        )

    def own_copy(part):
        return pltpu.make_async_copy(
            sources[part].at[:, head_columns(me)],
            rows_buf.at[me, :, pl.ds(part * HEAD_DIM, HEAD_DIM)],
            sem_recv.at[part, me],
        )

    def out_copy(target, origin):
        return pltpu.make_async_remote_copy(
            src_ref=out_buf.at[target],
            dst_ref=out_ref.at[:, head_columns(origin)],
            send_sem=sem_out_send.at[target],
            recv_sem=sem_out_recv.at[origin],
            device_id=device_of(target),
            device_id_type=pl.DeviceIdType.MESH,
        )

    def own_out():
        return pltpu.make_async_copy(
            out_buf.at[me], out_ref.at[:, head_columns(me)], sem_out_send.at[me]
        )

    for part in range(3):
        own_copy(part).start()

    barrier = pltpu.get_barrier_semaphore()

    def greet(away, shift):
        pl.semaphore_signal(
            barrier,
            inc=1,
            device_id=device_of(peer(away, shift)),
            device_id_type=pl.DeviceIdType.MESH,
        )

    each_peer(greet)
    pl.semaphore_wait(barrier, count - 1)

    def send_first(away, shift):
        target = peer(away, shift)
        ids_copy(target, me).start()
        part_copy(0, target, me).start()

    each_peer(send_first)
    for part in (1, 2):
        each_peer(lambda away, shift: part_copy(part, peer(away, shift), me).start())

    v_slots[:, :, HEAD_DIM:] = jnp.ones(
        (dp_count, count * capacity, HEAD_DIM), jnp.bfloat16
    )
    before = (
        lax.broadcasted_iota(jnp.int32, (row_count, row_count), 0)
        < lax.broadcasted_iota(jnp.int32, (row_count, row_count), 1)
    ).astype(jnp.bfloat16)
    part_lane = lax.broadcasted_iota(jnp.int32, (1, HEAD_DIM), 1) < SEG_BIN

    def member_hits(origin):
        ids = ids_buf[origin]
        member = ids - ids // SEG_BIN * SEG_BIN
        return lax.broadcasted_iota(jnp.int32, (HEAD_DIM, row_count), 0) == member

    def marks_of(place, hits):
        return lax.dot_general(
            place, hits.astype(jnp.bfloat16), NT, preferred_element_type=jnp.float32
        )

    def placed_part(place, origin, part):
        rows = rows_buf[origin, :, part * HEAD_DIM : (part + 1) * HEAD_DIM]
        return jnp.dot(place, rows, preferred_element_type=jnp.float32)

    def by_bin(value):
        return value.astype(jnp.bfloat16).reshape((dp_count, capacity, HEAD_DIM))

    def slots_at(index):
        return pl.ds(pl.multiple_of(index * capacity, capacity), capacity)

    def place_k(origin):
        bins = ids_buf[origin] // SEG_BIN
        bin_hits = lax.broadcasted_iota(jnp.int32, (16, row_count), 0) == bins
        ranks = jnp.dot(
            bin_hits.astype(jnp.bfloat16), before, preferred_element_type=jnp.float32
        )
        rank = jnp.sum(jnp.where(bin_hits, ranks, 0.0), axis=0, keepdims=True)
        slot = bins * capacity + rank.astype(jnp.int32)
        place = (
            lax.broadcasted_iota(jnp.int32, (slot_count, row_count), 0) == slot
        ).astype(jnp.bfloat16)
        place_buf[origin] = place
        other_member = marks_of(place, jnp.logical_not(member_hits(origin)))
        k_marks = jnp.where(part_lane, 1.0 - other_member, 0.0)
        k_slots[:, slots_at(origin), :HEAD_DIM] = by_bin(placed_part(place, origin, 0))
        k_slots[:, slots_at(origin), HEAD_DIM:] = by_bin(k_marks)

    def place_v(origin):
        placed = placed_part(place_buf[origin], origin, 1)
        v_slots[:, slots_at(origin), :HEAD_DIM] = by_bin(placed)

    def place_q(origin, inner):
        place = place_buf[origin]
        own_member = marks_of(place, member_hits(origin))
        q_marks = jnp.where(part_lane, (own_member - 1.0) * EXCLUDED, 0.0)
        at = slice(inner * capacity, (inner + 1) * capacity)
        q_slots[:, at, :HEAD_DIM] = by_bin(placed_part(place, origin, 2))
        q_slots[:, at, HEAD_DIM:] = by_bin(q_marks)

    ids_buf[me] = ids_ref[...]
    own_copy(0).wait()
    place_k(me)

    def take_k(away, shift):
        origin = peer(away, -shift)
        ids_copy(me, origin).wait_recv()
        part_copy(0, me, origin).wait_recv()
        place_k(origin)

    each_peer(take_k)
    own_copy(1).wait()
    place_v(me)

    def take_v(away, shift):
        origin = peer(away, -shift)
        part_copy(1, me, origin).wait_recv()
        place_v(origin)

    each_peer(take_v)

    exponent_scale = 1.0 / (math.sqrt(HEAD_DIM) * math.log(2.0))
    group_slots = group * capacity

    def attend_group(away, turn):
        for inner in range(group):
            shift = turn * group + inner
            origin = peer(away, -shift)
            if away == 0 and inner == 0:

                @pl.when(turn == 0)
                def _():
                    own_copy(2).wait()

                @pl.when(turn > 0)
                def _():
                    part_copy(2, me, origin).wait_recv()
            else:
                part_copy(2, me, origin).wait_recv()
            place_q(origin, inner)

        @pl.loop(0, dp_count, unroll=8)
        def _(bin_index):
            query = q_slots[bin_index]
            scores = lax.dot_general(
                query, k_slots[bin_index], NT, preferred_element_type=jnp.float32
            )
            row_max = jnp.max(scores, axis=1, keepdims=True)
            weights = jnp.exp2((scores - row_max) * exponent_scale).astype(jnp.bfloat16)
            sums = jnp.dot(weights, v_slots[bin_index], preferred_element_type=jnp.float32)
            attended = (sums[:, :HEAD_DIM] / sums[:, HEAD_DIM:]).astype(jnp.bfloat16)
            factor = jnp.zeros((group_slots, HEAD_DIM), jnp.float32)
            for member in range(SEG_BIN):
                mark = query[:, HEAD_DIM + member : HEAD_DIM + member + 1].astype(jnp.float32)
                row = table_ref[pl.ds(bin_index * SEG_BIN + member, 1), :]
                factor = jnp.where(mark == 0.0, 1.0 + row, factor)
            mixed = (attended.astype(jnp.float32) * factor).astype(jnp.bfloat16)
            group_out[bin_index] = mixed

        for inner in range(group):
            target = peer(away, -(turn * group + inner))
            slots = group_out[:, inner * capacity : (inner + 1) * capacity, :].reshape(
                (slot_count, HEAD_DIM)
            )
            out_buf[target] = lax.dot_general(
                place_buf[target], slots, TN, preferred_element_type=jnp.float32
            ).astype(jnp.bfloat16)
            if away == 0 and inner == 0:

                @pl.when(turn == 0)
                def _():
                    own_out().start()

                @pl.when(turn > 0)
                def _():
                    out_copy(target, me).start()
            else:
                out_copy(target, me).start()

    @pl.loop(0, half // group)
    def _(turn):
        attend_group(0, turn)
        attend_group(1, turn)

    @pl.loop(1, count)
    def _(step):
        target = (me + step) % count
        ids_copy(target, me).wait_send()
        part_copy(0, target, me).wait_send()
        part_copy(1, target, me).wait_send()
        part_copy(2, target, me).wait_send()
        out_copy(target, me).wait_send()
        out_copy(me, target).wait_recv()

    own_out().wait()


def head_shards(query_rows, key_rows, value_rows, seg_ids, timesteps, w_mod):
    dp_count = lax.axis_size("dp")
    seq_count = lax.axis_size("seq")
    count = dp_count * seq_count
    row_count, width = query_rows.shape
    capacity = 2 * row_count // dp_count
    group = count // 4
    me = lax.axis_index("dp") * seq_count + lax.axis_index("seq")
    head_weights = lax.dynamic_slice_in_dim(w_mod, me * HEAD_DIM, HEAD_DIM, 1)
    scale_table = scale_rows_table(timesteps, head_weights)
    ids = seg_ids.reshape(1, row_count)
    vmem = pl.BlockSpec(memory_space=pltpu.VMEM)
    anywhere = pl.BlockSpec(memory_space=pl.ANY)
    slots = (dp_count, count * capacity, 2 * HEAD_DIM)
    return pl.pallas_call(
        functools.partial(head_kernel, (dp_count, seq_count, capacity, group)),
        out_shape=pltpu.VMEM((row_count, width), jnp.bfloat16),
        in_specs=[anywhere, anywhere, anywhere, vmem, vmem],
        out_specs=vmem,
        scratch_shapes=[
            pltpu.VMEM((count, row_count, 3 * HEAD_DIM), jnp.bfloat16),
            pltpu.VMEM((count, 1, row_count), jnp.int32),
            pltpu.VMEM((count, dp_count * capacity, row_count), jnp.bfloat16),
            pltpu.VMEM((dp_count, group * capacity, 2 * HEAD_DIM), jnp.bfloat16),
            pltpu.VMEM(slots, jnp.bfloat16),
            pltpu.VMEM(slots, jnp.bfloat16),
            pltpu.VMEM((dp_count, group * capacity, HEAD_DIM), jnp.bfloat16),
            pltpu.VMEM((count, row_count, HEAD_DIM), jnp.bfloat16),
            pltpu.SemaphoreType.DMA((4, count)),
            pltpu.SemaphoreType.DMA((4, count)),
            pltpu.SemaphoreType.DMA((count,)),
            pltpu.SemaphoreType.DMA((count,)),
        ],
        compiler_params=pltpu.CompilerParams(
            collective_id=0, has_side_effects=True, vmem_limit_bytes=56 * 1024 * 1024
        ),
    )(query_rows, key_rows, value_rows, ids, scale_table)


def shards(query_rows, key_rows, value_rows, seg_ids, timesteps, w_mod):
    count = lax.axis_size("dp") * lax.axis_size("seq")
    whole_heads = query_rows.shape[1] == count * HEAD_DIM
    body = head_shards if whole_heads else routed_shards
    return body(query_rows, key_rows, value_rows, seg_ids, timesteps, w_mod)


def solution(mesh):
    placed = (
        P(("dp", "seq"), None),
        P(("dp", "seq"), None),
        P(("dp", "seq"), None),
        P(("dp", "seq")),
        P(),
        P(),
    )
    return jax.shard_map(
        shards, mesh=mesh, in_specs=placed, out_specs=P(("dp", "seq"), None), check_vma=False
    )
```
